32 devices in a mesh: depth: 4 (over y, x), chan: 8 (over z, core).
Axes of the slice: x: 2, y: 2, z: 4, core: 2. Of those that a mesh axis runs over, the one named last changes fastest.
Arguments:
- volume: float32 [512, 16, 1024], P('chan', 'depth'), may hold values from -6 to 6
- conv_weight: float32 [1, 3, 16, 32, 864], P(None, None, 'chan'), may hold values from -0.21875 to 0.21875
- norm_gain: float32 [1, 512], replicated, may hold values from 0.1 to 1.9
- mlp_in: float32 [1, 1024, 512], replicated, may hold values from -0.25 to 0.25
- mlp_out: float32 [1, 512, 1024], replicated, may hold values from -0.1875 to 0.1875
Outputs:
- features: float32 [512, 16, 1024], P('chan', 'depth')
The draws below stay inside these ranges and needn't reach their ends.
All inputs are finite; a program needn't handle non-finite values.
Results may differ from the reference program's by a relative error of at most 0.0001.
Values sent between devices are 32-bit elements; how exact they have to be, the bound alone decides.
A program may use at most 64 MiB of HBM per device.

```python
import jax
import jax.numpy as jnp
from jax import lax

C = 512
CG = 32
HID = 1024
H = 32
W = 32
BLOCKS = 1
CONVS = 3
GROUPS = 16
TAPS = 864
NZ = 16
HW = 1024


def block_scale(rng, dims, shards, least, top_value):
    gain = 1.0
    for position, parts in shards:
        draws = jax.random.uniform(jax.random.fold_in(jax.random.fold_in(rng, 6), position), (parts,), jnp.float32, least / len(shards), top_value / len(shards))
        gain = gain * jnp.repeat(jnp.exp(draws), dims[position] // parts).reshape((-1,) + (1,) * (len(dims) - 1 - position))
    return gain


def normal_values(rng, shape, deviation, bound, pieces=(), held_as=jnp.bfloat16):
    entries = deviation * jax.random.normal(rng, shape, jnp.float32)
    if pieces:
        entries = entries * block_scale(rng, shape, pieces, -0.22, 0.18)
    return jnp.clip(entries, -bound, bound).astype(held_as)


def setup_inputs(seed: int = 0) -> dict:
    keys = jax.random.split(jax.random.key(seed), 6)
    return {
        "volume": normal_values(keys[0], (C, NZ, HW), 1.0, 6.0, ((0, 8), (1, 4)), jnp.float32),
        "conv_weight": normal_values(keys[1], (BLOCKS, CONVS, GROUPS, CG, TAPS), TAPS ** -0.5, 0.21875, ((2, 8),), jnp.float32),
        "norm_gain": jnp.clip(1.0 + 0.18 * jax.random.normal(keys[2], (BLOCKS, C), jnp.float32), 0.1, 1.9),
        "mlp_in": normal_values(keys[3], (BLOCKS, HID, C), C ** -0.5, 0.25, (), jnp.float32),
        "mlp_out": normal_values(keys[4], (BLOCKS, C, HID), HID ** -0.5, 0.1875, (), jnp.float32),
    }


def convolve(field, kernel):
    grouped = field.reshape(GROUPS, CG, NZ, H, W)
    total = jnp.zeros_like(grouped)
    for shift_h in range(3):
        for shift_w in range(3):
            for shift_d in range(3):
                moved = jnp.roll(grouped, (1 - shift_d, 1 - shift_h, 1 - shift_w), (2, 3, 4))
                start = ((shift_h * 3 + shift_w) * 3 + shift_d) * CG
                piece = kernel[:, :, start:start + CG]
                total = total + jnp.einsum('goi,gizhw->gozhw', piece, moved, precision=lax.Precision.HIGHEST)
    return total.reshape(C, NZ, H * W)

def reference(volume, conv_weight, norm_gain, mlp_in, mlp_out):
    state = volume
    for block in range(BLOCKS):
        inner = jax.nn.gelu(convolve(state, conv_weight[block, 0]))
        inner = jax.nn.gelu(convolve(inner, conv_weight[block, 1]))
        mixed = state + convolve(inner, conv_weight[block, 2])
        flat = mixed.reshape(C, -1)
        scaled = flat * lax.rsqrt(lax.optimization_barrier(jnp.mean(flat * flat, axis=0)) + 1e-06) * norm_gain[block][:, None]
        hidden = jax.nn.gelu(jnp.dot(mlp_in[block], scaled, precision=lax.Precision.HIGHEST))
        flat = flat + jnp.dot(mlp_out[block], hidden, precision=lax.Precision.HIGHEST)
        state = flat.reshape(C, NZ, H * W)
    return state
```

```python
import functools

import jax
import jax.numpy as jnp
from jax import lax
from jax.experimental import pallas as pl
from jax.experimental.pallas import tpu as pltpu
from jax.sharding import PartitionSpec as P

W = 32
LIMIT = 60 * 1024 * 1024


def split(x):
    hi = x.astype(jnp.bfloat16)
    return hi, (x - hi.astype(jnp.float32)).astype(jnp.bfloat16)


def dot3(a, b):
    a_hi, a_lo = a
    b_hi, b_lo = b
    dot = functools.partial(jnp.dot, preferred_element_type=jnp.float32)
    return dot(a_hi, b_hi) + (dot(a_hi, b_lo) + dot(a_lo, b_hi))


def conv_body(last, chunk, *refs):
    if last:
        own, up, down, res, w, out, wf, wb, xb, acc = refs
    else:
        own, up, down, w, out, wf, wb, xb, acc = refs
        res = None
    planes, width, cells = own.shape
    deep = (planes + 2) * width
    span = 3 * deep

    @pl.when(pl.program_id(0) == 0)
    def _():
        wf[...] = jnp.zeros_like(wf)

    for b in range(3):
        for c in range(3):
            start = (b * 3 + c) * 3 * width
            piece = w[0, :, start : start + 3 * width]
            hi = piece.astype(jnp.bfloat16).astype(jnp.float32)
            lo = piece - hi
            for z in range(planes):
                row = (b * planes + z) * width
                for part, value in enumerate((hi, hi, lo)):
                    col = part * span + c * deep + z * width
                    wf[row : row + width, col : col + 3 * width] = value
    wb[...] = wf[...].astype(jnp.bfloat16)

    column = lax.broadcasted_iota(jnp.int32, (width, cells), 1) % W
    for z in range(planes + 2):
        x = up[0] if z == 0 else down[0] if z == planes + 1 else own[z - 1]
        before = jnp.where(column == 0, pltpu.roll(x, cells + 1 - W, 1), pltpu.roll(x, 1, 1))
        after = jnp.where(column == W - 1, pltpu.roll(x, W - 1, 1), pltpu.roll(x, cells - 1, 1))
        for c, value in enumerate((before, x, after)):
            hi, lo = split(value)
            row = c * deep + z * width
            xb[row : row + width, :] = hi
            xb[span + row : span + row + width, :] = lo
            xb[2 * span + row : 2 * span + row + width, :] = hi

    step = min(256, cells)
    for n in range(0, cells, step):
        acc[:, n : n + step] = jnp.dot(
            wb[...], xb[:, n : n + step], preferred_element_type=jnp.float32
        )

    for z in range(planes):
        p0, p1, p2 = (acc[(b * planes + z) * width : (b * planes + z + 1) * width, :] for b in range(3))
        value = p1 + pltpu.roll(p0, W, 1) + pltpu.roll(p2, cells - W, 1)
        if last:
            value = value + res[z]
            per = cells // chunk
            for q in range(per):
                out[z * per + q] = value[:, q * chunk : (q + 1) * chunk]
        else:
            out[z] = jax.nn.gelu(value)


def conv(own, up, down, kernel, res=None, chunk=None):
    planes, channels, cells = own.shape
    groups, width, taps = kernel.shape
    last = res is not None
    rows = 3 * planes * width
    span = 9 * (planes + 2) * width
    slab = pl.BlockSpec((planes, width, cells), lambda g: (0, g, 0))
    edge = pl.BlockSpec((1, width, cells), lambda g: (0, g, 0))
    weights = pl.BlockSpec((1, width, taps), lambda g: (g, 0, 0))
    if last:
        parts = planes * cells // chunk
        out_shape = (parts, channels, chunk)
        out_spec = pl.BlockSpec((parts, width, chunk), lambda g: (0, g, 0))
        args, specs = (own, up, down, res, kernel), [slab, edge, edge, slab, weights]
    else:
        out_shape, out_spec = own.shape, slab
        args, specs = (own, up, down, kernel), [slab, edge, edge, weights]
    return pl.pallas_call(
        functools.partial(conv_body, last, chunk),
        grid=(groups,),
        in_specs=specs,
        out_specs=out_spec,
        out_shape=jax.ShapeDtypeStruct(out_shape, jnp.float32),
        scratch_shapes=[
            pltpu.VMEM((rows, span), jnp.float32),
            pltpu.VMEM((rows, span), jnp.bfloat16),
            pltpu.VMEM((span, cells), jnp.bfloat16),
            pltpu.VMEM((rows, cells), jnp.float32),
        ],
        compiler_params=pltpu.CompilerParams(vmem_limit_bytes=LIMIT),
        name="conv",
    )(*args)


def mlp_body(x_ref, gain, w_in, w_out, out, r_hi, r_lo):
    @pl.when(pl.program_id(0) == 0)
    def _():
        x = x_ref[...]
        r = x * lax.rsqrt(jnp.mean(x * x, axis=0, keepdims=True) + 1e-06) * gain[...]
        hi, lo = split(r)
        r_hi[...] = hi
        r_lo[...] = lo
        out[...] = x

    hidden = jax.nn.gelu(dot3(split(w_in[...]), (r_hi[...], r_lo[...])))
    out[...] += dot3(split(w_out[...]), split(hidden))


def mlp(x, gain, w_in, w_out):
    channels, cells = x.shape
    hid = w_in.shape[0]
    block = min(256, hid)
    whole = pl.BlockSpec((channels, cells), lambda k: (0, 0))
    return pl.pallas_call(
        mlp_body,
        grid=(hid // block,),
        in_specs=[
            whole,
            pl.BlockSpec((channels, 1), lambda k: (0, 0)),
            pl.BlockSpec((block, channels), lambda k: (k, 0)),
            pl.BlockSpec((channels, block), lambda k: (0, k)),
        ],
        out_specs=whole,
        out_shape=jax.ShapeDtypeStruct(x.shape, jnp.float32),
        scratch_shapes=[pltpu.VMEM(x.shape, jnp.bfloat16)] * 2,
        compiler_params=pltpu.CompilerParams(vmem_limit_bytes=LIMIT),
        name="mlp",
    )(x, gain.reshape(-1, 1), w_in, w_out)


def edges(slab):
    count = lax.axis_size("depth")
    up = lax.ppermute(slab[-1:], "depth", [(i, (i + 1) % count) for i in range(count)])
    down = lax.ppermute(slab[:1], "depth", [((i + 1) % count, i) for i in range(count)])
    return up, down


def per_device(volume, conv_weight, norm_gain, mlp_in, mlp_out):
    channels, planes, cells = volume.shape
    count = lax.axis_size("chan")
    chunk = planes * cells // count
    slab = jnp.swapaxes(volume, 0, 1)
    kernels = conv_weight[0]
    inner = conv(slab, *edges(slab), kernels[0])
    inner = conv(inner, *edges(inner), kernels[1])
    mixed = conv(inner, *edges(inner), kernels[2], slab, chunk)
    runs = lax.all_to_all(mixed, "chan", split_axis=0, concat_axis=0, tiled=True)
    done = mlp(runs.reshape(count * channels, chunk), norm_gain[0], mlp_in[0], mlp_out[0])
    back = lax.all_to_all(
        done.reshape(count, channels, chunk), "chan", split_axis=0, concat_axis=0, tiled=True
    )
    back = back.reshape(planes, cells // chunk, channels, chunk)
    return back.transpose(2, 0, 1, 3).reshape(volume.shape)


def solution(mesh):
    in_specs = (P("chan", "depth", None), P(None, None, "chan", None, None), P(), P(), P())
    out_specs = P("chan", "depth", None)
    return jax.shard_map(
        per_device, mesh=mesh, in_specs=in_specs, out_specs=out_specs, check_vma=False
    )
```
